32 devices in a mesh: cols: 16 (over z, y, x), rows: 2 (over core).
Axes of the slice: x: 2, y: 2, z: 4, core: 2. Of those that a mesh axis runs over, the one named last changes fastest.
Arguments:
- vectors: float32 [2048, 4096], P('rows', 'cols'), may hold values from -6 to 6
- reflectors: float32 [3, 1024, 512], P(None, None, 'cols'), may hold values from -40 to 40, as said below
- factors: float32 [3, 512, 512], P(None, None, 'cols'), may hold values from -1 to 1
Outputs:
- result: float32 [2048, 4096], P('rows', 'cols')
The draws below stay inside these ranges and needn't reach their ends.
Inputs may be any that keep to these rules, and one draw needn't show every extreme that they name: `reflectors`: column j of each block is zero outside its rows j to j + 511, and its entry in row j is 1.
All inputs are finite; a program needn't handle non-finite values.
Results may differ from the reference program's by a relative error of at most 0.00028.
Values sent between devices are 32-bit elements; how exact they have to be, the bound alone decides.
No kernel may reach another device: no remote copies, remote signals or barrier semaphores. Data moves between devices by JAX's collectives and lax.ppermute only.
A program may use at most 64 MiB of HBM per device.

```python
import jax
import jax.numpy as jnp
from jax import lax

B = 512
BLOCKS = 3
NR = 2048
NC = 4096


def basis_draw(key):
    inner = jax.random.fold_in(key, 11)
    values = jax.random.normal(inner, (BLOCKS, 2 * B, B), jnp.float32)
    row_ids = lax.broadcasted_iota(jnp.int32, (2 * B, B), 0)
    col_ids = lax.broadcasted_iota(jnp.int32, (2 * B, B), 1)
    inside = (row_ids >= col_ids) & (row_ids < col_ids + B)
    leading = row_ids == col_ids
    banded = jnp.where(inside[None], values, jnp.float32(0.0))
    return jnp.where(leading[None], jnp.float32(1.0), banded)


def factor_from(basis_cols):
    gram = jnp.dot(basis_cols.T, basis_cols, precision=lax.Precision.HIGHEST, preferred_element_type=jnp.float32)
    upper = jnp.triu(gram, 1) + jnp.diag(jnp.diag(gram) * 0.5)
    return jnp.triu(jnp.linalg.inv(upper))


def draw_reflectors(key, part):
    return basis_draw(key)


def draw_factors(key, part):
    return jax.vmap(factor_from)(basis_draw(key))


def block_scale(own_key, dims, shards, least, high):
    factor_of, own = 1.0, jax.random.fold_in(own_key, 6)
    for dim, parts in shards:
        draws = jnp.exp(jax.random.uniform(jax.random.fold_in(own, dim), (parts,), jnp.float32, least / len(shards), high / len(shards)))
        factor_of = factor_of * jnp.repeat(draws, dims[dim] // parts).reshape([-1 if axis == dim else 1 for axis in range(len(dims))])
    return factor_of


def bell_draw(key, shape, scale, reach, pieces=(), dtype=jnp.bfloat16):
    drawn = jax.random.normal(key, shape, jnp.float32) * scale
    if len(pieces) > 0:
        drawn = block_scale(key, shape, pieces, -0.22, 0.18) * drawn
    return jnp.clip(drawn, min=-reach, max=reach).astype(dtype)


def setup_inputs(seed: int = 0) -> dict:
    key_list = jax.random.split(jax.random.key(seed), 4)
    return {
        "vectors": bell_draw(key_list[0], (NR, NC), 1.0, 6.0, ((0, 2), (1, 16)), jnp.float32),
        "reflectors": draw_reflectors(jax.random.fold_in(key_list[3], 71), 0),
        "factors": draw_factors(jax.random.fold_in(key_list[3], 71), 0),
    }


def reflect(window, basis_cols, factor):
    highest = lax.Precision.HIGHEST
    weights = jnp.dot(basis_cols.T.astype(jnp.float32), window.astype(jnp.float32), precision=highest, preferred_element_type=jnp.float32)
    coeffs = jnp.dot(factor.astype(jnp.float32), weights.astype(jnp.float32), precision=highest, preferred_element_type=jnp.float32)
    return window - jnp.dot(basis_cols.astype(jnp.float32), coeffs.astype(jnp.float32), precision=highest, preferred_element_type=jnp.float32)

def reference(vectors, reflectors, factors):

    def advance(index, matrix):
        start = (index * B).astype(jnp.int32)
        window = lax.dynamic_slice_in_dim(matrix, start, 2 * B, 0)
        basis_cols = lax.dynamic_index_in_dim(reflectors, index, 0, keepdims=False)
        factor = lax.dynamic_index_in_dim(factors, index, 0, keepdims=False)
        updated = reflect(window, basis_cols, factor)
        return lax.dynamic_update_slice_in_dim(matrix, updated, start, 0)
    return lax.fori_loop(0, BLOCKS, advance, vectors)
```

```python
import functools

import jax
import jax.numpy as jnp
from jax import lax
from jax.experimental import pallas as pl
from jax.experimental.pallas import tpu as pltpu
from jax.sharding import PartitionSpec as P


def shifted(value, axis, by):
    length = lax.axis_size(axis)
    pairs = [(i, i + by) for i in range(length) if 0 <= i + by < length]
    return lax.ppermute(value, axis, pairs)


def reflect(window, basis_cols, factor):
    highest = lax.Precision.HIGHEST
    weights = lax.dot_general(
        basis_cols,
        window,
        (((0,), (0,)), ((), ())),
        precision=highest,
        preferred_element_type=jnp.float32,
    )
    coeffs = jnp.dot(factor, weights, precision=highest, preferred_element_type=jnp.float32)
    return window - jnp.dot(
        basis_cols, coeffs, precision=highest, preferred_element_type=jnp.float32
    )


def pipeline_body(vectors, reflectors, factors):
    row_count = lax.axis_size("rows")
    row_index = lax.axis_index("rows")
    half_rows = vectors.shape[0] // 2
    first_index = jnp.maximum(2 * row_index - 1, 0)
    pick = lambda array, index: lax.dynamic_index_in_dim(array, index, 0, keepdims=False)
    pair_basis = jnp.stack([pick(reflectors, first_index), pick(reflectors, 2 * row_index)])
    pair_factor = jnp.stack([pick(factors, first_index), pick(factors, 2 * row_index)])
    full_basis = lax.all_gather(pair_basis, "cols", axis=2, tiled=True)
    full_factor = lax.all_gather(pair_factor, "cols", axis=2, tiled=True)
    has_upper = row_index > 0
    has_lower = row_index < row_count - 1

    def advance(turn, state_now):
        matrix, outgoing, returning = state_now
        incoming = shifted(outgoing, "rows", 1)
        arrived = shifted(returning, "rows", -1)
        landing = (turn - row_index - 2 == 0) & has_lower
        lower = jnp.where(landing, arrived, matrix[half_rows:])
        matrix = jnp.concatenate([matrix[:half_rows], lower], 0)

        def busy(state_in):
            stripe = state_in[0]
            window = reflect(
                jnp.concatenate([incoming, stripe[:half_rows]], 0), full_basis[0], full_factor[0]
            )
            upper_rows = jnp.where(has_upper, window[half_rows:], stripe[:half_rows])
            stripe = reflect(
                jnp.concatenate([upper_rows, stripe[half_rows:]], 0),
                full_basis[1],
                full_factor[1],
            )
            return (stripe, stripe[half_rows:], window[:half_rows])

        state = (matrix, outgoing, returning)
        return lax.cond(turn == row_index, busy, lambda state_in: state_in, state)

    blank = jnp.zeros((half_rows, vectors.shape[1]), jnp.float32)
    return lax.fori_loop(0, row_count + 1, advance, (vectors, blank, blank))[0]


def dot_nn(a, b):
    return lax.dot_general(a, b, (((1,), (0,)), ((), ())), preferred_element_type=jnp.float32)


def dot_nt(a, b):
    return lax.dot_general(a, b, (((1,), (1,)), ((), ())), preferred_element_type=jnp.float32)


def split(value):
    high = value.astype(jnp.bfloat16)
    low = (value - high.astype(jnp.float32)).astype(jnp.bfloat16)
    return high, low


def unpack(place_ref, own_ref, other_ref, vh, vl, fh, fl):
    count, part, width = own_ref.shape
    cols = fh.shape[1]
    me, core = place_ref[0], place_ref[1]
    row_ids = lax.broadcasted_iota(jnp.int32, (part, width), 1)
    col_ids = lax.broadcasted_iota(jnp.int32, (part, width), 0)
    for step in range(count):
        source = lax.bitwise_xor(me, step % 4 * 4 + step // 4)
        for ref, half in ((own_ref, core), (other_ref, 1 - core)):
            first = pl.multiple_of((source * 2 + half) * part, part)
            rows = pl.ds(first, part)
            packed = ref[step]
            diff = row_ids - (col_ids + first)
            basis = jnp.where(diff > 0, packed, jnp.where(diff == 0, 1.0, 0.0))
            vh[rows, :], vl[rows, :] = split(basis)
            factor = jnp.where(diff[:, :cols] <= 0, packed[:, :cols], 0.0)
            fh[rows, :], fl[rows, :] = split(factor)


def reflect_rows(window, vh, vl, fh, fl):
    wide, cols = window.shape[1], fh.shape[1]
    half = cols // 2
    xh, xl = split(window)
    weights = []
    for first in (0, half):
        rows = slice(first, first + wide - half)
        cs = slice(first, first + half)
        weights.append(
            dot_nt(xh[:, rows], vh[cs, rows])
            + dot_nt(xh[:, rows], vl[cs, rows])
            + dot_nt(xl[:, rows], vh[cs, rows])
        )
    wh, wl = split(jnp.concatenate(weights, 1))
    coeffs = []
    for first in (0, half):
        cs, rs = slice(first, cols), slice(first, first + half)
        coeffs.append(
            dot_nn(wh[:, cs], fh[cs, rs])
            + dot_nn(wh[:, cs], fl[cs, rs])
            + dot_nn(wl[:, cs], fh[cs, rs])
        )
    zh, zl = split(jnp.concatenate(coeffs, 1))
    outs = []
    for index in range(wide // half):
        rs = slice(index * half, (index + 1) * half)
        cs = slice(0, half) if index == 0 else slice(half, cols)
        if 0 < index < wide // half - 1:
            cs = slice(0, cols)
        outs.append(
            dot_nn(zh[:, cs], vh[cs, rs])
            + dot_nn(zh[:, cs], vl[cs, rs])
            + dot_nn(zl[:, cs], vh[cs, rs])
        )
    return window - jnp.concatenate(outs, 1)


def middle_kernel(place_ref, own_ref, other_ref, top_ref, low_ref, top_out, low_out, vh, vl, fh, fl):
    unpack(place_ref, own_ref, other_ref, vh, vl, fh, fl)
    window = jnp.concatenate([top_ref[...], low_ref[...]], 1)
    cols = fh.shape[1]
    window = reflect_rows(window, vh, vl, fh, fl)
    top_out[...] = window[:, :cols]
    low_out[...] = window[:, cols:]


def last_kernel(
    place_ref, own_ref, other_ref, top_ref, low_ref, first_ref, second_ref, out, vh, vl, fh, fl
):
    cols = fh.shape[1]

    @pl.when(place_ref[1] == 0)
    def _():
        out[:cols, :] = first_ref[...].T
        out[cols:, :] = second_ref[...].T

    @pl.when(place_ref[1] == 1)
    def _():
        unpack(place_ref, own_ref, other_ref, vh, vl, fh, fl)
        window = jnp.concatenate([top_ref[...], low_ref[...]], 1)
        window = reflect_rows(window, vh, vl, fh, fl)
        out[...] = window.T


def call(kernel, shapes, args, block):
    cols, wide = block
    vmem = pl.BlockSpec(memory_space=pltpu.VMEM)
    flops = 2 * 3 * args[3].shape[0] * cols * (2 * wide + cols)
    size = sum(a.size for a in args) * 4
    return pl.pallas_call(
        kernel,
        out_shape=shapes,
        in_specs=[pl.BlockSpec(memory_space=pltpu.SMEM)] + [vmem] * (len(args) - 1),
        out_specs=jax.tree.map(lambda _: vmem, shapes),
        scratch_shapes=[
            pltpu.VMEM((cols, wide), jnp.bfloat16),
            pltpu.VMEM((cols, wide), jnp.bfloat16),
            pltpu.VMEM((cols, cols), jnp.bfloat16),
            pltpu.VMEM((cols, cols), jnp.bfloat16),
        ],
        compiler_params=pltpu.CompilerParams(vmem_limit_bytes=40 * 1024 * 1024),
        cost_estimate=pl.CostEstimate(flops=flops, bytes_accessed=size, transcendentals=0),
    )(*args)


def paired_body(vectors, reflectors, factors):
    count = lax.axis_size("cols")
    me = lax.axis_index("cols")
    core = lax.axis_index("rows")
    blocks, wide, shard = reflectors.shape
    cols = factors.shape[1]
    part = shard // 2
    place = jnp.stack([me, core]).astype(jnp.int32)

    def flip(value, mask):
        return lax.ppermute(value, "cols", [(i, i ^ mask) for i in range(count)])

    def across(value):
        return lax.ppermute(value, "rows", [(0, 1), (1, 0)])

    basis = jnp.swapaxes(reflectors, 1, 2)
    factor = jnp.pad(jnp.swapaxes(factors, 1, 2), ((0, 0), (0, 0), (0, wide - cols)))
    row_ids = lax.broadcasted_iota(jnp.int32, basis.shape, 2)
    col_ids = lax.broadcasted_iota(jnp.int32, basis.shape, 1) + me * shard
    packed = jnp.where(row_ids <= col_ids, factor, basis)
    mine = lax.dynamic_slice_in_dim(packed, core * part, part, 1)

    turned = vectors.T
    others = across(turned)
    half = lambda value, index: value[:, index * cols : (index + 1) * cols]
    is_top = core == 0
    chunks = [
        jnp.where(is_top, half(turned, 0), half(others, 0)),
        jnp.where(is_top, half(turned, 1), half(others, 1)),
        jnp.where(is_top, half(others, 0), half(turned, 0)),
        half(turned, 1),
    ]

    gathered = []
    for k in range(blocks):
        own = mine[k]
        column = jnp.stack([own] + [flip(own, 4 * d) for d in range(1, count // 4)])
        by_x = flip(column, 1)
        by_y = flip(column, 2)
        mid = column.shape[0] // 2
        corner = [flip(by_x[:mid], 2), flip(by_y[mid:], 1)]
        plane = jnp.concatenate([column, by_x, by_y] + corner, 0)
        gathered.append((plane, across(plane)))

    shape = jax.ShapeDtypeStruct((vectors.shape[1], cols), jnp.float32)
    for k in range(blocks - 1):
        chunks[k], chunks[k + 1] = call(
            middle_kernel,
            (shape, shape),
            (place, *gathered[k], chunks[k], chunks[k + 1]),
            (cols, wide),
        )
    last = blocks - 1
    return call(
        last_kernel,
        jax.ShapeDtypeStruct(vectors.shape, jnp.float32),
        (place, *gathered[last], chunks[last], chunks[last + 1], chunks[0], chunks[1]),
        (cols, wide),
    )


def solution(mesh):
    placed = (P("rows", "cols"), P(None, None, "cols"), P(None, None, "cols"))
    paired = mesh.shape["rows"] == 2 and mesh.shape["cols"] == 16
    return jax.shard_map(
        paired_body if paired else pipeline_body,
        mesh=mesh,
        in_specs=placed,
        out_specs=P("rows", "cols"),
        check_vma=False,
    )
```

```python
import functools

import jax
import jax.numpy as jnp
from jax import lax
from jax.experimental import pallas as pl
from jax.experimental.pallas import tpu as pltpu
from jax.sharding import PartitionSpec as P


def shifted(value, axis, by):
    length = lax.axis_size(axis)
    pairs = [(i, i + by) for i in range(length) if 0 <= i + by < length]
    return lax.ppermute(value, axis, pairs)


def reflect(window, basis_cols, factor):
    highest = lax.Precision.HIGHEST
    weights = lax.dot_general(
        basis_cols,
        window,
        (((0,), (0,)), ((), ())),
        precision=highest,
        preferred_element_type=jnp.float32,
    )
    coeffs = jnp.dot(factor, weights, precision=highest, preferred_element_type=jnp.float32)
    return window - jnp.dot(
        basis_cols, coeffs, precision=highest, preferred_element_type=jnp.float32
    )


def pipeline_body(vectors, reflectors, factors):
    row_count = lax.axis_size("rows")
    row_index = lax.axis_index("rows")
    half_rows = vectors.shape[0] // 2
    first_index = jnp.maximum(2 * row_index - 1, 0)
    pick = lambda array, index: lax.dynamic_index_in_dim(array, index, 0, keepdims=False)
    pair_basis = jnp.stack([pick(reflectors, first_index), pick(reflectors, 2 * row_index)])
    pair_factor = jnp.stack([pick(factors, first_index), pick(factors, 2 * row_index)])
    full_basis = lax.all_gather(pair_basis, "cols", axis=2, tiled=True)
    full_factor = lax.all_gather(pair_factor, "cols", axis=2, tiled=True)
    has_upper = row_index > 0
    has_lower = row_index < row_count - 1

    def advance(turn, state_now):
        matrix, outgoing, returning = state_now
        incoming = shifted(outgoing, "rows", 1)
        arrived = shifted(returning, "rows", -1)
        landing = (turn - row_index - 2 == 0) & has_lower
        lower = jnp.where(landing, arrived, matrix[half_rows:])
        matrix = jnp.concatenate([matrix[:half_rows], lower], 0)

        def busy(state_in):
            stripe = state_in[0]
            window = reflect(
                jnp.concatenate([incoming, stripe[:half_rows]], 0), full_basis[0], full_factor[0]
            )
            upper_rows = jnp.where(has_upper, window[half_rows:], stripe[:half_rows])
            stripe = reflect(
                jnp.concatenate([upper_rows, stripe[half_rows:]], 0),
                full_basis[1],
                full_factor[1],
            )
            return (stripe, stripe[half_rows:], window[:half_rows])

        state = (matrix, outgoing, returning)
        return lax.cond(turn == row_index, busy, lambda state_in: state_in, state)

    blank = jnp.zeros((half_rows, vectors.shape[1]), jnp.float32)
    return lax.fori_loop(0, row_count + 1, advance, (vectors, blank, blank))[0]


def dot_nn(a, b):
    return lax.dot_general(a, b, (((1,), (0,)), ((), ())), preferred_element_type=jnp.float32)


def dot_nt(a, b):
    return lax.dot_general(a, b, (((1,), (1,)), ((), ())), preferred_element_type=jnp.float32)


def split(value):
    high = value.astype(jnp.bfloat16)
    low = (value - high.astype(jnp.float32)).astype(jnp.bfloat16)
    return high, low


def unpack(orders, place_ref, refs, vh, vl, fh, fl):
    near, far, near_other, far_other = refs
    count, part, width = near.shape
    cols = fh.shape[1]
    me, core = place_ref[0], place_ref[1]
    row_ids = lax.broadcasted_iota(jnp.int32, (part, width), 1)
    col_ids = lax.broadcasted_iota(jnp.int32, (part, width), 0)
    for step in range(2 * count):
        for pair, half in (((near, far), core), ((near_other, far_other), 1 - core)):
            flips = [
                functools.reduce(lambda a, b: a ^ b, [m for p, m in enumerate(o) if step >> p & 1], 0)
                for o in orders
            ]
            source = lax.bitwise_xor(me, jnp.where(half == 0, flips[0], flips[1]))
            first = pl.multiple_of((source * 2 + half) * part, part)
            rows = pl.ds(first, part)
            packed = pair[step // count][step % count]
            diff = row_ids - (col_ids + first)
            basis = jnp.where(diff > 0, packed, jnp.where(diff == 0, 1.0, 0.0))
            vh[rows, :], vl[rows, :] = split(basis)
            factor = jnp.where(diff[:, :cols] <= 0, packed[:, :cols], 0.0)
            fh[rows, :], fl[rows, :] = split(factor)


def reflect_rows(window, vh, vl, fh, fl):
    wide, cols = window.shape[1], fh.shape[1]
    half = cols // 2
    xh, xl = split(window)
    weights = []
    for first in (0, half):
        rows = slice(first, first + wide - half)
        cs = slice(first, first + half)
        weights.append(
            dot_nt(xh[:, rows], vh[cs, rows])
            + dot_nt(xh[:, rows], vl[cs, rows])
            + dot_nt(xl[:, rows], vh[cs, rows])
        )
    wh, wl = split(jnp.concatenate(weights, 1))
    coeffs = []
    for first in (0, half):
        cs, rs = slice(first, cols), slice(first, first + half)
        coeffs.append(
            dot_nn(wh[:, cs], fh[cs, rs])
            + dot_nn(wh[:, cs], fl[cs, rs])
            + dot_nn(wl[:, cs], fh[cs, rs])
        )
    zh, zl = split(jnp.concatenate(coeffs, 1))
    outs = []
    for index in range(wide // half):
        rs = slice(index * half, (index + 1) * half)
        cs = slice(0, half) if index == 0 else slice(half, cols)
        if 0 < index < wide // half - 1:
            cs = slice(0, cols)
        outs.append(
            dot_nn(zh[:, cs], vh[cs, rs])
            + dot_nn(zh[:, cs], vl[cs, rs])
            + dot_nn(zl[:, cs], vh[cs, rs])
        )
    return window - jnp.concatenate(outs, 1)


def pick_rows(place_ref, own_ref, other_ref, owner, rows):
    return jnp.where(place_ref[1] == owner, own_ref[rows, :], other_ref[rows, :]).T


def first_kernel(orders, place_ref, *refs):
    *planes, own_ref, other_ref, top_out, low_out, vh, vl, fh, fl = refs
    unpack(orders, place_ref, planes, vh, vl, fh, fl)
    window = pick_rows(place_ref, own_ref, other_ref, 0, slice(None))
    window = reflect_rows(window, vh, vl, fh, fl)
    cols = fh.shape[1]
    top_out[...] = window[:, :cols].T
    low_out[...] = window[:, cols:]


def middle_kernel(orders, place_ref, *refs):
    *planes, top_ref, own_ref, other_ref, top_out, low_out, vh, vl, fh, fl = refs
    cols = fh.shape[1]
    unpack(orders, place_ref, planes, vh, vl, fh, fl)
    low = pick_rows(place_ref, own_ref, other_ref, 1, slice(0, cols))
    window = jnp.concatenate([top_ref[...], low], 1)
    window = reflect_rows(window, vh, vl, fh, fl)
    top_out[...] = window[:, :cols].T
    low_out[...] = window[:, cols:]


def last_kernel(orders, place_ref, *refs):
    *planes, top_ref, own_ref, first_ref, second_ref, out, vh, vl, fh, fl = refs
    cols = fh.shape[1]

    @pl.when(place_ref[1] == 0)
    def _():
        out[:cols, :] = first_ref[...]
        out[cols:, :] = second_ref[...]

    @pl.when(place_ref[1] == 1)
    def _():
        unpack(orders, place_ref, planes, vh, vl, fh, fl)
        window = jnp.concatenate([top_ref[...], own_ref[cols:, :].T], 1)
        window = reflect_rows(window, vh, vl, fh, fl)
        out[...] = window.T


def call(kernel, shapes, args, block):
    cols, wide = block
    vmem = pl.BlockSpec(memory_space=pltpu.VMEM)
    flops = 2 * 3 * 256 * cols * (2 * wide + cols)
    size = sum(a.size for a in args) * 4
    return pl.pallas_call(
        kernel,
        out_shape=shapes,
        in_specs=[pl.BlockSpec(memory_space=pltpu.SMEM)] + [vmem] * (len(args) - 1),
        out_specs=jax.tree.map(lambda _: vmem, shapes),
        scratch_shapes=[
            pltpu.VMEM((cols, wide), jnp.bfloat16),
            pltpu.VMEM((cols, wide), jnp.bfloat16),
            pltpu.VMEM((cols, cols), jnp.bfloat16),
            pltpu.VMEM((cols, cols), jnp.bfloat16),
        ],
        compiler_params=pltpu.CompilerParams(vmem_limit_bytes=24 * 1024 * 1024),
        cost_estimate=pl.CostEstimate(flops=flops, bytes_accessed=size, transcendentals=0),
    )(*args)


def exchange_orders(blocks, count):
    x, y, near, far = 1, 2, 4, 8
    early = ((far, near, x, y), (near, far, y, x))
    late = ((x, far, near, y), (y, near, far, x))
    return [early] * (blocks - 1) + [late]


def paired_body(vectors, reflectors, factors):
    count = lax.axis_size("cols")
    me = lax.axis_index("cols")
    core = lax.axis_index("rows")
    blocks, wide, shard = reflectors.shape
    cols = factors.shape[1]
    part = shard // 2
    place = jnp.stack([me, core]).astype(jnp.int32)
    orders = exchange_orders(blocks, count)

    def exchange(value, k, step):
        masks = [orders[k][c][step] for c in range(2)]
        pairs = [(2 * i + c, 2 * (i ^ masks[c]) + c) for i in range(count) for c in range(2)]
        with jax.named_scope(f"step_{k}_{step}"):
            return lax.ppermute(value, ("cols", "rows"), pairs)

    def across(value, name):
        with jax.named_scope(name):
            return lax.ppermute(value, "rows", [(0, 1), (1, 0)])

    basis = jnp.swapaxes(reflectors, 1, 2)
    factor = jnp.pad(jnp.swapaxes(factors, 1, 2), ((0, 0), (0, 0), (0, wide - cols)))
    row_ids = lax.broadcasted_iota(jnp.int32, basis.shape, 2)
    col_ids = lax.broadcasted_iota(jnp.int32, basis.shape, 1) + me * shard
    packed = jnp.where(row_ids <= col_ids, factor, basis)
    mine = lax.dynamic_slice_in_dim(packed, core * part, part, 1)
    others = across(vectors, "rows_x")

    gathered = []
    for k in range(blocks):
        held = mine[k][None]
        for step in range(3):
            held = jnp.concatenate([held, exchange(held, k, step)], 0)
        near_other = across(held, f"rows_{k}_near")
        far = exchange(held, k, 3)
        far_other = across(far, f"rows_{k}_far")
        gathered.append((held, far, near_other, far_other))

    natural = jax.ShapeDtypeStruct((cols, vectors.shape[1]), jnp.float32)
    turned = jax.ShapeDtypeStruct((vectors.shape[1], cols), jnp.float32)
    block = (cols, wide)
    first, low = call(
        functools.partial(first_kernel, orders[0]),
        (natural, turned),
        (place, *gathered[0], vectors, others),
        block,
    )
    second, low = call(
        functools.partial(middle_kernel, orders[1]),
        (natural, turned),
        (place, *gathered[1], low, vectors, others),
        block,
    )
    return call(
        functools.partial(last_kernel, orders[2]),
        jax.ShapeDtypeStruct(vectors.shape, jnp.float32),
        (place, *gathered[2], low, vectors, first, second),
        block,
    )


def solution(mesh):
    placed = (P("rows", "cols"), P(None, None, "cols"), P(None, None, "cols"))
    paired = mesh.shape["rows"] == 2 and mesh.shape["cols"] == 16
    return jax.shard_map(
        paired_body if paired else pipeline_body,
        mesh=mesh,
        in_specs=placed,
        out_specs=P("rows", "cols"),
        check_vma=False,
    )
```
